32 devices in a mesh: row: 4 (over x, core), col: 8 (over z, y).
Axes of the slice: x: 2, y: 2, z: 4, core: 2. Of those that a mesh axis runs over, the one named last changes fastest.
Arguments:
- pair_density: bfloat16 [2048, 8192], P('col', 'row'), may hold values from -6 to 6
- scale_exp: int32 [2048], replicated, may hold values from -1 to 1
- pair_weight: int32 [2048], replicated, may hold values from 1 to 4
- resident_ids: int32 [512], replicated, may hold values from 0 to 2047, as said below
- diagonal_shift: float32 [8192], replicated, may hold values from 2 to 4
- background: float32 [8192, 8192], P('row', 'col'), as said below
Outputs:
- dielectric: float32 [8192, 8192], P('row', 'col')
- kernel: float32 [2048, 512], P(('col', 'row'))
The draws below stay inside these ranges and needn't reach their ends.
Inputs may be any that keep to these rules, and one draw needn't show every extreme that they name: `resident_ids`: 512 distinct pair indices. background is symmetric.
All inputs are finite; a program needn't handle non-finite values.
Results may differ from the reference program's by a relative error of at most 0.0003.
Values may be sent and summed in bfloat16 or wider, within the bound.
No kernel may reach another device: no remote copies, remote signals or barrier semaphores. Data moves between devices by JAX's collectives and lax.ppermute only.
A program may use at most 128 MiB of HBM per device.

```python
import math
import jax
import jax.numpy as jnp
from jax import lax

NG = 8192
NRES = 512
SWEEPS = 2
NPAIR = 2048


def draw_background(key, part):
    normal_draw = jax.random.normal(jax.random.fold_in(key, 11), (NG, NG), jnp.float32)
    return (normal_draw + normal_draw.T) * (0.35 / math.sqrt(NG))


def draw_resident_ids(key, part):
    middle_ids = jax.random.permutation(jax.random.fold_in(key, 7), NPAIR - 2)[:NRES - 2] + 1
    chosen = jnp.concatenate([middle_ids.astype(jnp.int32), jnp.array([0, NPAIR - 1], jnp.int32)])
    shuffle = jax.random.permutation(jax.random.fold_in(key, 8), NRES)
    return chosen[shuffle].astype(jnp.int32)


def touch_ends(drawn, stream_key, least, top_value):
    extent = drawn.shape
    index_at = [jax.random.randint(jax.random.fold_in(stream_key, axis), (), 0, extent[axis]) for axis in range(len(extent))]
    drawn = drawn.at[tuple(index_at)].set(least)
    longest = extent.index(max(extent))
    index_at[longest] = (index_at[longest] + 1) % extent[longest]
    return drawn.at[tuple(index_at)].set(top_value)


def block_scale(own_key, shape, cuts, smallest, top_value):
    def one(axis_at, blocks):
        draws = jax.random.uniform(jax.random.fold_in(jax.random.fold_in(own_key, 6), axis_at), (blocks,), jnp.float32, smallest / len(cuts), top_value / len(cuts))
        return jnp.repeat(jnp.exp(draws), shape[axis_at] // blocks).reshape((-1,) + (1,) * (len(shape) - axis_at - 1))

    gain = one(*cuts[0])
    for cut in cuts[1:]:
        gain = gain * one(*cut)
    return gain


def noise(stream_key, shape, spread, bound, split=(), kind=jnp.bfloat16):
    result = jax.random.normal(stream_key, shape, jnp.float32) * spread
    if len(split) > 0:
        result = block_scale(stream_key, shape, split, -0.22, 0.18) * result
    return jnp.clip(result, min=-bound, max=bound).astype(kind)


def setup_inputs(seed: int = 0) -> dict:
    seeds = jax.random.split(jax.random.key(seed), 7)
    pair_density = noise(seeds[0], (NPAIR, NG), 1.0, 6.0, ((0, 8), (1, 4)))
    scale_exp = touch_ends(jax.random.randint(seeds[1], (NPAIR,), -1, 2), jax.random.fold_in(seeds[1], 1), -1, 1).astype(jnp.int32)
    pair_weight = touch_ends(jax.random.randint(seeds[2], (NPAIR,), 1, 5), jax.random.fold_in(seeds[2], 1), 1, 4).astype(jnp.int32)
    resident_ids = draw_resident_ids(jax.random.fold_in(seeds[6], 71), 0)
    diagonal_shift = jnp.clip(jnp.exp(jax.random.uniform(seeds[4], (NG,), jnp.float32, math.log(2.0), math.log(4.0))), 2.0, 4.0)
    background = draw_background(jax.random.fold_in(seeds[6], 71), 0)
    return dict(pair_density=pair_density, scale_exp=scale_exp, pair_weight=pair_weight, resident_ids=resident_ids, diagonal_shift=diagonal_shift, background=background)


damping = 0.5

def scale_factor(exponent):
    return jnp.where(exponent < 0, 0.5, jnp.where(exponent > 0, 2.0, 1.0)).astype(jnp.float32)

def reference(pair_density, scale_exp, pair_weight, resident_ids, diagonal_shift, background):
    factor = scale_factor(scale_exp)
    scaled = (pair_density.astype(jnp.float32) * factor[:, None]).astype(jnp.bfloat16)
    response = lax.dot_general(scaled, scaled, (((0,), (0,)), ((), ())), preferred_element_type=jnp.float32) / (4 * NPAIR)
    dielectric = background + response + jnp.diag(diagonal_shift)
    wide_scaled = scaled.astype(jnp.float32)
    precond = diagonal_shift + jnp.einsum('pg,pg->g', wide_scaled, wide_scaled) / (4 * NPAIR)
    source = pair_density[resident_ids].astype(jnp.float32).T
    screened = source / precond[:, None]
    for sweep_index in range(SWEEPS):
        image = jnp.dot(dielectric, screened, precision=lax.Precision.HIGHEST)
        screened = screened + damping * (source - image) / precond[:, None]
    product = jnp.dot(pair_density.astype(jnp.float32), screened, precision=lax.Precision.HIGHEST)
    kernel = pair_weight.astype(jnp.float32)[:, None] * product / math.sqrt(NG)
    return (dielectric, kernel)
```

```python
import math

import jax
import jax.numpy as jnp
from jax import lax
from jax.sharding import PartitionSpec as P


AXES = ("row", "col")
F32 = jnp.float32
BF16 = jnp.bfloat16


def scale_factor(exponent):
    return jnp.where(exponent < 0, 0.5, jnp.where(exponent > 0, 2.0, 1.0)).astype(F32)


def contract(left, right):
    return lax.dot_general(left, right, (((0,), (0,)), ((), ())), preferred_element_type=F32)


def matmul(left, right):
    return jnp.dot(left, right, preferred_element_type=F32)


def split_two(value):
    high = lax.reduce_precision(value, 8, 7)
    return high.astype(BF16), (value - high).astype(BF16)


def shards(pair_density, scale_exp, pair_weight, resident_ids, diagonal_shift, background):
    rows, cols = lax.axis_size("row"), lax.axis_size("col")
    row, col = lax.axis_index("row"), lax.axis_index("col")
    pair_dev, row_width = pair_density.shape
    col_width = background.shape[1]
    pair_total = pair_dev * cols
    grid_total = row_width * rows
    norm = 1.0 / (4 * pair_total)
    ratio = cols // rows
    root = col // ratio
    offset = (col % ratio) * col_width

    def hop(value, row_mask, col_mask, keep=None):
        pairs = [
            (r * cols + c, (r ^ row_mask) * cols + (c ^ col_mask))
            for r in range(rows)
            for c in range(cols)
            if keep is None or keep(r, c)
        ]
        return lax.ppermute(value, AXES, pairs)

    def over_row(value):
        done = 0
        mask = rows // 2
        while mask:
            def holds(r, c, done=done):
                return (r ^ (c // ratio)) & ~done == 0

            moved = hop(value, mask, 0, holds)
            value = jnp.where((row ^ root) & mask != 0, moved, value)
            done |= mask
            mask //= 2
        return value

    def own_columns(value):
        return lax.dynamic_slice_in_dim(value, offset, col_width, value.ndim - 1)

    factor = scale_factor(scale_exp)
    own_factor = lax.dynamic_slice_in_dim(factor, col * pair_dev, pair_dev)
    scaled = (pair_density.astype(F32) * own_factor[:, None]).astype(BF16)

    squares = jnp.sum(jnp.square(scaled.astype(F32)), axis=0)
    mask = 1
    while mask < cols:
        squares = squares + hop(squares, 0, mask)
        mask *= 2
    row_start = row * row_width
    col_start = col * col_width
    shift_rows = lax.dynamic_slice_in_dim(diagonal_shift, row_start, row_width)
    precond_rows = shift_rows + squares * norm
    precond_cols = over_row(own_columns(precond_rows))

    half = pair_dev // 2
    halves = [scaled[:half], scaled[half:]]
    units = [dict() for _ in range(2)]
    for h in range(2):
        units[h][0] = halves[h]
    steps = cols // 2
    for h in range(2):
        u = units[h]
        u[1] = hop(u[0], 0, 1)
        for m in range(1, steps, 2):
            u[2 * m] = hop(u[0], 0, 2 * m)
            u[2 * m + 1] = hop(u[2 * m], 0, 1)
        for m in range(2, steps, 2):
            u[2 * m] = hop(u[2 * (m ^ 1)], 0, 2)
            if h == 0:
                u[2 * m + 1] = hop(u[2 * m], 0, 1)
            else:
                u[2 * m + 1] = hop(u[2 * (m ^ 1) + 1], 0, 2)
    order = [0, 1] + [2 * m + b for m in range(1, steps, 2) for b in range(2)]
    order += [2 * m + b for m in range(2, steps, 2) for b in range(2)]
    left = [jnp.concatenate([units[0][m], units[1][m]]) for m in order]
    right = [over_row(own_columns(piece)) for piece in left]

    def one_hot(m):
        start = (col ^ m) * pair_dev
        ids = start + lax.broadcasted_iota(jnp.int32, (pair_dev, resident_ids.shape[0]), 0)
        inverse = 1.0 / lax.dynamic_slice_in_dim(factor, start, pair_dev)
        return jnp.where(ids == resident_ids[None, :], inverse[:, None], 0.0).astype(BF16)

    picks = jnp.concatenate([one_hot(m) for m in order])
    cut = len(order) // 2
    response = background
    response = response + contract(jnp.concatenate(left[:cut]), jnp.concatenate(right[:cut])) * norm
    response = response + contract(jnp.concatenate(left[cut:]), jnp.concatenate(right[cut:])) * norm
    left_all = jnp.concatenate(left)
    right_all = jnp.concatenate(right)
    global_rows = row_start + lax.broadcasted_iota(jnp.int32, (row_width, col_width), 0)
    global_cols = col_start + lax.broadcasted_iota(jnp.int32, (row_width, col_width), 1)
    on_diagonal = global_rows == global_cols
    dielectric = response + jnp.where(on_diagonal, shift_rows[:, None], 0.0)
    inverse_rows = 1.0 / precond_rows
    inverse_cols = 1.0 / precond_cols
    coupling = (
        (dielectric - jnp.where(on_diagonal, precond_rows[:, None], 0.0)) * inverse_rows[:, None]
    ).astype(BF16)

    source_rows = contract(left_all, picks).astype(BF16)
    source_cols = contract(right_all, picks)

    image = contract(coupling, source_rows)
    core = row % 2
    part = col_width // 2
    kept = lax.dynamic_slice_in_dim(image, core * part, part)
    sent = lax.dynamic_slice_in_dim(image, (1 - core) * part, part)
    kept = kept + hop(sent, 1, 0)
    mask = 2
    while mask < rows:
        kept = kept + hop(kept, mask, 0)
        mask *= 2
    other = hop(kept, 1, 0)
    image = jnp.where(core == 0, jnp.concatenate([kept, other]), jnp.concatenate([other, kept]))
    screen = (source_cols - 0.5 * image) * inverse_cols[:, None]
    tail = (source_cols - 0.25 * image) * inverse_cols[:, None]

    screen_high, screen_low = split_two(screen)
    update = -0.5 * (matmul(coupling, screen_high) + matmul(coupling, screen_low))
    update_high, update_low = split_two(update)
    quarter = col_width // rows
    tail_high, tail_low = split_two(lax.dynamic_slice_in_dim(tail, row * quarter, quarter))
    right_part = lax.dynamic_slice_in_dim(right_all, row * quarter, quarter, 1)
    partial_value = (
        matmul(left_all, update_high)
        + matmul(left_all, update_low)
        + matmul(right_part, tail_high)
        + matmul(right_part, tail_low)
    )

    residents = resident_ids.shape[0]
    share = pair_dev // rows
    summed = partial_value.reshape(cols, rows // 2, 2, share, residents)
    kept = lax.dynamic_index_in_dim(summed, core, 2, False)
    sent = lax.dynamic_index_in_dim(summed, 1 - core, 2, False)
    summed = kept + hop(sent, 1, 0)
    mask = rows // 2
    while mask >= 2:
        bit = (row // mask) % 2
        summed = summed.reshape(cols, 2, -1, share, residents)
        kept = lax.dynamic_index_in_dim(summed, bit, 1, False)
        sent = lax.dynamic_index_in_dim(summed, 1 - bit, 1, False)
        summed = kept + hop(sent, mask, 0)
        mask //= 2
    summed = summed.reshape(cols, share, residents)
    place = {m: i for i, m in enumerate(order)}
    summed = summed.reshape(cols // 2, 2, share, residents)
    summed = summed[:, 0] + hop(summed[:, 1], 0, 1)
    lines = {m: summed[place[2 * m] // 2] for m in range(steps)}
    evens = [m for m in range(2, steps, 2)]
    if evens:
        moved = hop(jnp.stack([lines[m] for m in evens]), 0, 2)
        for i, m in enumerate(evens):
            lines[m ^ 1] = lines[m ^ 1] + moved[i]
    total = lines[0]
    for m in range(1, steps, 2):
        total = total + hop(lines[m], 0, 2 * m)
    mine = col * pair_dev + row * share
    weights = lax.dynamic_slice_in_dim(pair_weight, mine, share).astype(F32)
    scale = weights / lax.dynamic_slice_in_dim(factor, mine, share) / math.sqrt(grid_total)
    return dielectric, scale[:, None] * total


def solution(mesh):
    return jax.shard_map(
        shards,
        mesh=mesh,
        in_specs=(P("col", "row"), P(), P(), P(), P(), P("row", "col")),
        out_specs=(P("row", "col"), P(("col", "row"), None)),
        check_vma=False,
    )
```

```python
import functools
import math

import jax
import jax.numpy as jnp
from jax import lax
from jax.experimental import pallas as pl
from jax.experimental.pallas import tpu as pltpu
from jax.sharding import PartitionSpec as P


AXES = ("row", "col")
F32 = jnp.float32
F16 = jnp.float16
BF16 = jnp.bfloat16
CHUNKS = 2
HEAD = 16


def scale_factor(exponent):
    return jnp.where(exponent < 0, 0.5, jnp.where(exponent > 0, 2.0, 1.0)).astype(F32)


def contract(left, right):
    return lax.dot_general(left, right, (((0,), (0,)), ((), ())), preferred_element_type=F32)


def matmul(left, right):
    return jnp.dot(left, right, preferred_element_type=F32)


def pack(value):
    top = jnp.max(jnp.abs(value))
    power = jnp.clip(jnp.ceil(jnp.log2(jnp.maximum(top, 1e-30))), -100.0, 126.0)
    body = (value * jnp.exp2(12.0 - power)).astype(F16)
    return jnp.concatenate([body, jnp.full((HEAD, value.shape[1]), power, F32).astype(F16)])


def unpack(message):
    body = message[:-HEAD].astype(F32)
    return body * jnp.exp2(message[-1, 0].astype(F32) - 12.0)


def join(refs):
    return jnp.concatenate([ref[...] for ref in refs])


def accumulate_kernel(norm, counts, base_ref, seen_ref, *refs):
    lefts, rest = refs[: 2 * counts], refs[2 * counts :]
    rights, picks, (out_ref, source_ref) = rest[:-counts - 2], rest[-counts - 2 : -2], rest[-2:]
    left = join(lefts)
    out_ref[...] = base_ref[...] + contract(left, join(rights)) * norm
    found = contract(left, join(picks)).astype(BF16)
    source_ref[...] = found if seen_ref is None else seen_ref[...] + found


def first_kernel(norm, counts, base_ref, *refs):
    accumulate_kernel(norm, counts, base_ref, None, *refs)


def last_kernel(norm, counts, tile, place_ref, base_ref, seen_ref, shift_ref, precond_ref, *refs):
    lefts, rest = refs[: 2 * counts], refs[2 * counts :]
    rights, picks = rest[:-counts - 5], rest[-counts - 5 : -5]
    out_ref, coupling_ref, kept_ref, sent_ref, image_ref = rest[-5:]
    step = pl.program_id(0)

    @pl.when(step == 0)
    def _():
        image_ref[...] = jnp.zeros_like(image_ref)

    left = join(lefts)
    value = base_ref[...] + contract(left, join(rights)) * norm
    source = seen_ref[...] + contract(left, join(picks)).astype(BF16)
    shape = value.shape
    gap = place_ref[0] - place_ref[1] + step * tile
    across = lax.broadcasted_iota(jnp.int32, shape, 1) - lax.broadcasted_iota(jnp.int32, shape, 0)
    on_diagonal = across == gap
    value = value + jnp.where(on_diagonal, shift_ref[...], 0.0)
    out_ref[...] = value
    precond = precond_ref[:, :1]
    coupling = (value - jnp.where(on_diagonal, precond, 0.0)) * (1.0 / precond)
    coupling = coupling.astype(BF16)
    coupling_ref[...] = coupling
    image_ref[...] += contract(coupling, source)

    @pl.when(step == pl.num_programs(0) - 1)
    def _():
        core = place_ref[2]
        part, width = kept_ref.shape[1:]
        for j in range(kept_ref.shape[0]):
            lanes = slice(j * width, (j + 1) * width)
            kept_ref[j] = image_ref[pl.ds(pl.multiple_of(core * part, part), part), lanes]
            sent_ref[j] = image_ref[pl.ds(pl.multiple_of((1 - core) * part, part), part), lanes]


def split_two(value):
    high = value.astype(BF16)
    return high, (value - high.astype(F32)).astype(BF16)


def product_kernel(units, place_ref, coupling_ref, screen_ref, tail_ref, *refs):
    lefts, rest = refs[: 2 * units], refs[2 * units :]
    parts, (kept_ref, sent_ref, total_ref, screen_two) = rest[:-4], rest[-4:]
    step = pl.program_id(0)
    width = screen_ref.shape[1]

    @pl.when(step == 0)
    def _():
        high, low = split_two(screen_ref[...])
        screen_two[:, :width] = high
        screen_two[:, width:] = low
        high, low = split_two(tail_ref[...])
        start = 0
        for ref in parts:
            size = ref.shape[0]
            total_ref[start : start + size] = matmul(ref[...], high) + matmul(ref[...], low)
            start += size

    both = matmul(coupling_ref[...], screen_two[...])
    high, low = split_two(-0.5 * (both[:, :width] + both[:, width:]))
    half = lefts[0].shape[0]
    for u in range(units):
        left = join(lefts[2 * u : 2 * u + 2])
        total_ref[2 * u * half : 2 * (u + 1) * half] += matmul(left, high) + matmul(left, low)

    @pl.when(step == pl.num_programs(0) - 1)
    def _():
        core = place_ref[2]
        share = kept_ref.shape[2]
        for u in range(units):
            for x in range(kept_ref.shape[1]):
                base = 2 * u * half + 2 * x * share
                kept_ref[u, x] = total_ref[pl.ds(pl.multiple_of(base + core * share, share), share)]
                sent_ref[u, x] = total_ref[
                    pl.ds(pl.multiple_of(base + (1 - core) * share, share), share)
                ]


def const(shape):
    return pl.BlockSpec(shape, lambda i, *_: (0,) * len(shape))


def row_tiles(tile, width):
    return pl.BlockSpec((tile, width), lambda i, *_: (i, 0))


def lane_tiles(height, tile):
    return pl.BlockSpec((height, tile), lambda i, *_: (0, i))


def pick_spec(height, width, index):
    return pl.BlockSpec((height, width), lambda i, *_: (index, 0))


def cost(flops, moved):
    return pl.CostEstimate(flops=int(flops), bytes_accessed=int(moved), transcendentals=0)


def shards(pair_density, scale_exp, pair_weight, resident_ids, diagonal_shift, background):
    rows, cols = lax.axis_size("row"), lax.axis_size("col")
    row, col = lax.axis_index("row"), lax.axis_index("col")
    pair_dev, row_width = pair_density.shape
    col_width = background.shape[1]
    residents = resident_ids.shape[0]
    pair_total = pair_dev * cols
    grid_total = row_width * rows
    norm = 1.0 / (4 * pair_total)
    ratio = cols // rows
    root = col // ratio
    core = row % 2
    offset = (col % ratio) * col_width
    row_start = row * row_width
    col_start = col * col_width

    def hop(value, row_mask, col_mask, keep=None):
        pairs = [
            (r * cols + c, (r ^ row_mask) * cols + (c ^ col_mask))
            for r in range(rows)
            for c in range(cols)
            if keep is None or keep(r, c)
        ]
        return lax.ppermute(value, AXES, pairs)

    def over_row(value):
        done = 0
        mask = rows // 2
        while mask:
            def holds(r, c, done=done):
                return (r ^ (c // ratio)) & ~done == 0

            moved = hop(value, mask, 0, holds)
            value = jnp.where((row ^ root) & mask != 0, moved, value)
            done |= mask
            mask //= 2
        return value

    def own_columns(value):
        return lax.dynamic_slice_in_dim(value, offset, col_width, value.ndim - 1)

    factor = scale_factor(scale_exp)
    own_factor = lax.dynamic_slice_in_dim(factor, col * pair_dev, pair_dev)
    scaled = (pair_density.astype(F32) * own_factor[:, None]).astype(BF16)

    half = pair_dev // 2
    steps = cols // 2
    units = [{0: scaled[:half]}, {0: scaled[half:]}]
    for h in range(2):
        u = units[h]
        u[1] = hop(u[0], 0, 1)
        for m in range(1, steps, 2):
            own = u[0]
            if m > 1:
                own, _ = lax.optimization_barrier((own, u[2 * m - 4 if m > 3 else 2]))
            u[2 * m] = hop(own, 0, 2 * m)
            u[2 * m + 1] = hop(u[2 * m], 0, 1)
        for m in range(2, steps, 2):
            u[2 * m] = hop(u[2 * (m ^ 1)], 0, 2)
            if h == 0:
                u[2 * m + 1] = hop(u[2 * m], 0, 1)
            else:
                u[2 * m + 1] = hop(u[2 * (m ^ 1) + 1], 0, 2)
    lines = [0] + list(range(1, steps, 2)) + list(range(2, steps, 2))
    order = [2 * m + b for m in lines for b in range(2)]
    pieces = {m: [units[0][m], units[1][m]] for m in order}

    def columns_of(members):
        return over_row(jnp.concatenate([own_columns(p) for m in members for p in pieces[m]]))

    groups = [order[i : i + 2] for i in range(0, len(order), 2)]
    calls = [groups[:2], groups[2:-1], groups[-1:]]
    right = {}
    for g in groups[:-1]:
        right[tuple(g)] = columns_of(g)
    last = groups[-1]
    for m in last:
        right[(m,)] = columns_of([m])

    def one_hot(m):
        start = (col ^ m) * pair_dev
        ids = start + lax.broadcasted_iota(jnp.int32, (pair_dev, residents), 0)
        inverse = 1.0 / lax.dynamic_slice_in_dim(factor, start, pair_dev)
        return jnp.where(ids == resident_ids[None, :], inverse[:, None], 0.0).astype(BF16)

    picks = jnp.concatenate([one_hot(m) for m in order])

    def squares(pieces_of):
        return sum(jnp.sum(jnp.square(p.astype(F32)), axis=0) for p in pieces_of)

    shift_rows = lax.dynamic_slice_in_dim(diagonal_shift, row_start, row_width)
    shift_cols = lax.dynamic_slice_in_dim(diagonal_shift, col_start, col_width)
    precond_rows = shift_rows + squares([p for m in order for p in pieces[m]]) * norm
    precond_wide = jnp.broadcast_to(precond_rows[:, None], (row_width, 128))
    precond_cols = shift_cols + squares(right.values()) * norm
    inverse_cols = 1.0 / precond_cols

    place = jnp.stack([row_start, col_start, core]).astype(jnp.int32)
    tile = min(256, row_width)
    grid = row_width // tile
    value, source = background, None
    for index, call in enumerate(calls):
        members = [m for g in call for m in g]
        if not members:
            continue
        count = len(members)
        lefts = [p for m in members for p in pieces[m]]
        final = index == 2
        rights = [right[(m,)] for m in last] if final else [right[tuple(g)] for g in call]
        spots = [order.index(m) for m in members]
        in_specs = [row_tiles(tile, col_width)]
        operands = [value]
        if source is not None:
            in_specs.append(row_tiles(tile, residents))
            operands.append(source)
        if final:
            in_specs += [const((1, col_width)), row_tiles(tile, 128)]
            operands += [shift_cols[None, :], precond_wide]
        in_specs += [lane_tiles(half, tile)] * (2 * count)
        in_specs += [const(r.shape) for r in rights]
        in_specs += [pick_spec(pair_dev, residents, s) for s in spots]
        operands += lefts + rights + [picks] * count
        flops = 2 * row_width * count * pair_dev * (col_width + residents)
        moved = row_width * (8 * col_width + 4 * residents + 2 * count * pair_dev)
        out_specs = [row_tiles(tile, col_width)]
        out_shape = [jax.ShapeDtypeStruct((row_width, col_width), F32)]
        if not final:
            body = first_kernel if source is None else accumulate_kernel
            value, source = pl.pallas_call(
                functools.partial(body, norm, count),
                grid=(grid,),
                in_specs=in_specs,
                out_specs=out_specs + [row_tiles(tile, residents)],
                out_shape=out_shape + [jax.ShapeDtypeStruct((row_width, residents), BF16)],
                cost_estimate=cost(flops, moved),
            )(*operands)
            continue
        part, width = col_width // 2, residents // CHUNKS
        dielectric, coupling, image_kept, image_sent = pl.pallas_call(
            functools.partial(last_kernel, norm, count, tile),
            grid_spec=pltpu.PrefetchScalarGridSpec(
                num_scalar_prefetch=1,
                grid=(grid,),
                in_specs=in_specs,
                out_specs=out_specs
                + [row_tiles(tile, col_width)]
                + [const((CHUNKS, part, width))] * 2,
                scratch_shapes=[pltpu.VMEM((col_width, residents), F32)],
            ),
            out_shape=out_shape
            + [jax.ShapeDtypeStruct((row_width, col_width), BF16)]
            + [jax.ShapeDtypeStruct((CHUNKS, part, width), F32)] * 2,
            cost_estimate=cost(flops + 2 * row_width * col_width * residents, moved),
        )(place, *operands)

    right_list = [right[tuple(g)] for g in groups[:-1]] + [right[(m,)] for m in last]
    source_cols = 0.0
    start = 0
    for r in right_list:
        source_cols = source_cols + contract(r, picks[start : start + r.shape[0]])
        start += r.shape[0]
    quarter = col_width // rows
    right_parts = [lax.dynamic_slice_in_dim(r, row * quarter, quarter, 1) for r in right_list]
    all_lefts = [p for m in order for p in pieces[m]]
    tile = min(512, row_width)
    share = pair_dev // rows
    count = len(order)
    mine = col * pair_dev + row * share
    weights = lax.dynamic_slice_in_dim(pair_weight, mine, share).astype(F32)
    scale = weights / lax.dynamic_slice_in_dim(factor, mine, share) / math.sqrt(grid_total)

    kernel = []
    for j in range(CHUNKS):
        kept = image_kept[j] + hop(image_sent[j], 1, 0)
        mask = 2
        while mask < rows:
            kept = kept + unpack(hop(pack(kept), mask, 0))
            mask *= 2
        other = hop(kept, 1, 0)
        image = jnp.where(
            core == 0, jnp.concatenate([kept, other]), jnp.concatenate([other, kept])
        )
        found = source_cols[:, j * width : (j + 1) * width]
        screen = (found - 0.5 * image) * inverse_cols[:, None]
        tail = (found - 0.25 * image) * inverse_cols[:, None]
        tail = lax.dynamic_slice_in_dim(tail, row * quarter, quarter)
        shape = (count, rows // 2, share, width)
        kept, sent = pl.pallas_call(
            functools.partial(product_kernel, count),
            grid_spec=pltpu.PrefetchScalarGridSpec(
                num_scalar_prefetch=1,
                grid=(row_width // tile,),
                in_specs=[
                    row_tiles(tile, col_width),
                    const(screen.shape),
                    const(tail.shape),
                ]
                + [lane_tiles(half, tile)] * (2 * count)
                + [const(r.shape) for r in right_parts],
                out_specs=[const(shape)] * 2,
                scratch_shapes=[
                    pltpu.VMEM((pair_total, width), F32),
                    pltpu.VMEM((col_width, 2 * width), BF16),
                ],
            ),
            out_shape=[jax.ShapeDtypeStruct(shape, F32)] * 2,
            cost_estimate=cost(
                4 * row_width * width * (col_width + pair_total),
                2 * row_width * (col_width + pair_total),
            ),
        )(place, coupling, screen, tail, *all_lefts, *right_parts)

        summed = kept + hop(sent, 1, 0)
        mask = rows // 2
        while mask >= 2:
            bit = (row // mask) % 2
            summed = summed.reshape(count, 2, -1, share, width)
            kept = lax.dynamic_index_in_dim(summed, bit, 1, False)
            sent = lax.dynamic_index_in_dim(summed, 1 - bit, 1, False)
            moved = unpack(hop(pack(sent.reshape(-1, width)), mask, 0))
            summed = kept + moved.reshape(kept.shape)
            mask //= 2
        summed = summed.reshape(steps, 2, share, width)
        moved = unpack(hop(pack(summed[:, 1].reshape(-1, width)), 0, 1))
        summed = summed[:, 0] + moved.reshape(steps, share, width)
        total = summed[0]
        for i, m in enumerate(lines[1:]):
            total = total + unpack(hop(pack(summed[i + 1]), 0, 2 * m))
        kernel.append(scale[:, None] * total)
    return dielectric, jnp.concatenate(kernel, axis=1)


def solution(mesh):
    return jax.shard_map(
        shards,
        mesh=mesh,
        in_specs=(P("col", "row"), P(), P(), P(), P(), P("row", "col")),
        out_specs=(P("row", "col"), P(("col", "row"), None)),
        check_vma=False,
    )
```
